256 devices in a mesh: req: 64 (over y, z, core), mlp: 4 (over x).
Axes of the slice: x: 4, y: 4, z: 8, core: 2. Of those that a mesh axis runs over, the one named last changes fastest.
Arguments:
- queries: bfloat16 [64, 2, 16, 2, 1536], P('req', None, 'mlp'), may hold values from -64 to 64
- new_kv: bfloat16 [64, 2, 16, 2, 256], P('req', None, 'mlp'), may hold values from -9 to 9
- residual: bfloat16 [64, 2, 16, 2, 1536], P('req', None, 'mlp'), may hold values from -3 to 3
- prompt_kv: bfloat16 [64, 1024, 256], P('req'), may hold values from -9 to 9
- tail_kv: bfloat16 [64, 16, 64, 256], P('req', 'mlp'), may hold values from -9 to 9
- page_pool: bfloat16 [16384, 20, 256], P(('req', 'mlp')), may hold values from -9 to 9
- page_holder: int32 [256, 64], P(('req', 'mlp')), may hold values from 0 to 63, as said below
- serve_slot: int32 [256, 64], P(('req', 'mlp')), may hold values from 0 to 63
- prompt_len: int32 [64, 2], P('req'), may hold values from 512 to 32768
- tail_len: int32 [64, 2, 16], P('req', None, 'mlp'), may hold values from 1 to 62, 496 in all within a row
- w_out: bfloat16 [1536, 1536], P('mlp'), may hold values from -0.15625 to 0.15625
- norm_mlp: float32 [1536], replicated, may hold values from 0.25 to 1.75
- w_gate: bfloat16 [1536, 4608], P(None, 'mlp'), may hold values from -0.15625 to 0.15625
- w_up: bfloat16 [1536, 4608], P(None, 'mlp'), may hold values from -0.15625 to 0.15625
- w_down: bfloat16 [4608, 1536], P('mlp'), may hold values from -0.09375 to 0.09375
- norm_final: float32 [1536], replicated, may hold values from 0.25 to 1.75
- w_score: float32 [1536], replicated, may hold values from -0.15625 to 0.15625
Outputs:
- scores: float32 [64, 2, 16, 2], P('req', None, 'mlp')
- hidden_out: bfloat16 [64, 2, 16, 2, 1536], P('req', None, 'mlp')
- tails_out: bfloat16 [64, 2, 16, 64, 256], P('req', None, 'mlp')
The draws below stay inside these ranges and needn't reach their ends.
Inputs may be any that keep to these rules, and one draw needn't show every extreme that they name: Each row of page_holder names every req index once.
All inputs are finite; a program needn't handle non-finite values. No bound on the sum of `tail_len` on one device may be relied on, other than what follows from the above.
Results may differ from the reference program's by a relative error of at most 0.015.
Values may be sent and summed in bfloat16 or wider, within the bound.
No kernel may reach another device: no remote copies, remote signals or barrier semaphores. Data moves between devices by JAX's collectives and lax.ppermute only.
A program may use at most 64 MiB of HBM per device.

```python
import math
import jax
import jax.numpy as jnp
import numpy as np
from jax import lax

D = 1536
FF = 4608
H = 12
HD = 128
WIN = 1024
SAMPLES = 16
TAIL = 64
PAGE = 20
N_REQ = 64
N_MLP = 4


def draw_queries(key, part):
    shape = (N_REQ, 2, SAMPLES, 2, H * HD)
    base = jnp.clip(jax.random.normal(jax.random.fold_in(key, 11), shape, jnp.float32), -4.0, 4.0)
    return base.astype(jnp.bfloat16)


def draw_page_holder(key, part):
    keys = jax.random.split(jax.random.fold_in(key, 21), N_REQ * N_MLP)
    table = jax.vmap(lambda k: jax.random.permutation(k, N_REQ))(keys)
    return table.astype(jnp.int32)


def place_ends(array, own_key, least, top_value):
    longest = array.shape.index(max(array.shape))
    spots = []
    for shift in (0, 1):
        where = [jax.random.randint(jax.random.fold_in(own_key, axis), (), 0, length) for axis, length in enumerate(array.shape)]
        where[longest] = (where[longest] + shift) % array.shape[longest]
        spots.append(tuple(where))
    return array.at[spots[0]].set(least).at[spots[1]].set(top_value)


def steps_of(key, extent, pieces, low, top_value):
    def one(position, parts):
        draws = jax.random.uniform(jax.random.fold_in(jax.random.fold_in(key, 6), position), (parts,), jnp.float32, low / len(pieces), top_value / len(pieces))
        return jnp.repeat(jnp.exp(draws), extent[position] // parts).reshape((-1,) + (1,) * (len(extent) - position - 1))

    factor_of = one(*pieces[0])
    for cut in pieces[1:]:
        factor_of = factor_of * one(*cut)
    return factor_of


def split_up(count, total, bound, lean):
    weights = [(1 << 20) // math.isqrt(grade ** lean) + 1 for grade in range(2, count + 1)]
    spare, holding = total - bound - (count - 1), [1] * (count - 1)
    while spare > 0:
        candidates = [i for i in range(count - 1) if holding[i] < bound]
        pool, remaining = sum([weights[i] for i in candidates]), spare
        for i in candidates:
            extra = min(bound - holding[i], max(1, remaining * weights[i] // pool), spare)
            holding[i] = holding[i] + extra
            spare = spare - extra
    return np.array([bound] + holding)


def ragged(key, amount, total, most, slope):
    if amount == 2:
        one = jax.random.randint(key, (), max(1, total - most), min(most, total - 1) + 1)
        return jnp.stack([one, total - one])
    tallies = jnp.asarray(split_up(amount, total, most, slope), jnp.int32)
    twos = (amount - 1) // 2
    source_of, sink = tallies[1:1 + 2 * twos:2], tallies[2:2 + 2 * twos:2]
    slack = jnp.minimum(source_of - 1, most - sink)
    passed = jax.random.randint(jax.random.fold_in(key, 1), (twos,), 0, 1 << 20) % (slack + 1)
    tallies = tallies.at[1:1 + 2 * twos:2].set(source_of - passed).at[2:2 + 2 * twos:2].set(sink + passed)
    return tallies[jax.random.permutation(jax.random.fold_in(key, 2), amount)]


def noise(rng, dims, spread, reach, cuts=(), kind=jnp.bfloat16):
    entries = jax.random.normal(rng, dims, jnp.float32) * spread
    if len(cuts) > 0:
        entries = steps_of(rng, dims, cuts, -0.22, 0.18) * entries
    return jnp.clip(entries, min=-reach, max=reach).astype(kind)


def setup_inputs(seed: int = 0) -> dict:
    key_of = jax.random.split(jax.random.key(seed), 18)
    return {
        "queries": draw_queries(jax.random.fold_in(key_of[17], 71), 0),
        "new_kv": noise(key_of[1], (N_REQ, 2, SAMPLES, 2, 2 * HD), 1.5, 9.0, ((0, 64), (2, 4))),
        "residual": noise(key_of[2], (N_REQ, 2, SAMPLES, 2, D), 0.5, 3.0, ((0, 64), (2, 4))),
        "prompt_kv": noise(key_of[3], (N_REQ, WIN, 2 * HD), 1.5, 9.0, ((0, 64),)),
        "tail_kv": noise(key_of[4], (N_REQ, SAMPLES, TAIL, 2 * HD), 1.5, 9.0, ((0, 64), (1, 4))),
        "page_pool": noise(key_of[5], (N_REQ * N_MLP * N_REQ, PAGE, 2 * HD), 1.5, 9.0, ((0, 256),)),
        "page_holder": draw_page_holder(jax.random.fold_in(key_of[17], 71), 0),
        "serve_slot": place_ends(jax.random.randint(key_of[7], (N_REQ * N_MLP, N_REQ), 0, N_REQ), jax.random.fold_in(key_of[7], 1), 0, N_REQ - 1).astype(jnp.int32),
        "prompt_len": place_ends(jax.random.randint(key_of[8], (N_REQ, 2), WIN // 2, 32 * WIN + 1), jax.random.fold_in(key_of[8], 1), WIN // 2, 32 * WIN).astype(jnp.int32),
        "tail_len": jax.vmap(lambda own: ragged(own, SAMPLES, SAMPLES * (TAIL - 2) // 2, TAIL - 2, 2))(jax.random.split(key_of[9], N_REQ * 2)).reshape((N_REQ, 2, SAMPLES)).astype(jnp.int32),
        "w_out": noise(key_of[10], (H * HD, D), (H * HD) ** -0.5, 0.15625, ((0, 4),)),
        "norm_mlp": jnp.clip(1.0 + 0.15 * jax.random.normal(key_of[11], (D,), jnp.float32), 0.25, 1.75),
        "w_gate": noise(key_of[12], (D, FF), D ** -0.5, 0.15625, ((1, 4),)),
        "w_up": noise(key_of[13], (D, FF), D ** -0.5, 0.15625, ((1, 4),)),
        "w_down": noise(key_of[14], (FF, D), FF ** -0.5, 0.09375, ((0, 4),)),
        "norm_final": jnp.clip(1.0 + 0.15 * jax.random.normal(key_of[15], (D,), jnp.float32), 0.25, 1.75),
        "w_score": noise(key_of[16], (D,), D ** -0.5, 0.15625, (), jnp.float32),
    }


def attend(query, fresh, window, tails, plen, tlen):
    count = query.shape[0]
    size = window.shape[-1] // 2
    q = query.reshape(count, 2, -1, size).astype(jnp.float32)
    scale = 1.0 / jnp.sqrt(jnp.float32(size))
    wk = window[:, :size].astype(jnp.float32)
    wv = window[:, size:].astype(jnp.float32)
    tk = tails[..., :size].astype(jnp.float32)
    tv = tails[..., size:].astype(jnp.float32)
    nk = fresh[..., :size].astype(jnp.float32)
    nv = fresh[..., size:].astype(jnp.float32)
    s_win = jnp.einsum('sthd,kd->sthk', q, wk) * scale
    s_tail = jnp.einsum('sthd,sjd->sthj', q, tk) * scale
    s_new = jnp.einsum('sthd,sud->sthu', q, nk) * scale
    tpos = tlen[:, None] + jnp.arange(2, dtype=jnp.int32)[None, :]
    kw = jnp.arange(window.shape[0], dtype=jnp.int32)[None, None, None, :]
    ok_win = (kw >= window.shape[0] - plen) & (kw > tpos[:, :, None, None])
    kt = jnp.arange(tails.shape[1], dtype=jnp.int32)[None, None, None, :]
    ok_tail = kt < tlen[:, None, None, None]
    steps = jnp.arange(2, dtype=jnp.int32)
    ok_new = steps[None, None, None, :] <= steps[None, :, None, None]
    s_win = jnp.where(ok_win, s_win, -1e+30)
    s_tail = jnp.where(ok_tail, s_tail, -1e+30)
    s_new = jnp.where(ok_new, s_new, -1e+30)
    top = jnp.maximum(jnp.maximum(s_win.max(-1), s_tail.max(-1)), s_new.max(-1))[..., None]
    e_win = jnp.where(ok_win, jnp.exp(s_win - top), 0.0)
    e_tail = jnp.where(ok_tail, jnp.exp(s_tail - top), 0.0)
    e_new = jnp.where(ok_new, jnp.exp(s_new - top), 0.0)
    total = e_win.sum(-1, keepdims=True) + e_tail.sum(-1, keepdims=True) + e_new.sum(-1, keepdims=True)
    p_win = (e_win / total).astype(jnp.bfloat16).astype(jnp.float32)
    p_tail = (e_tail / total).astype(jnp.bfloat16).astype(jnp.float32)
    p_new = (e_new / total).astype(jnp.bfloat16).astype(jnp.float32)
    out = jnp.einsum('sthk,kd->sthd', p_win, wv)
    out = out + jnp.einsum('sthj,sjd->sthd', p_tail, tv)
    out = out + jnp.einsum('sthu,sud->sthd', p_new, nv)
    return out.reshape(count, 2, -1).astype(jnp.bfloat16)

def extend(tails, fresh, tlen):
    rows = jnp.arange(tails.shape[1], dtype=jnp.int32)[None, :, None]
    lead = tlen[:, None, None]
    out = jnp.where(rows == lead, fresh[:, 0][:, None, :], tails)
    return jnp.where(rows == lead + 1, fresh[:, 1][:, None, :], out)

def rms_scale(values):
    return values * lax.rsqrt(lax.optimization_barrier(jnp.mean(values * values, axis=-1, keepdims=True)) + 1e-06)

def reference(queries, new_kv, residual, prompt_kv, tail_kv, page_pool, page_holder, serve_slot, prompt_len, tail_len, w_out, norm_mlp, w_gate, w_up, w_down, norm_final, w_score):
    samp_dev = SAMPLES // N_MLP
    rows = WIN + samp_dev * TAIL
    holder = page_holder.reshape(N_REQ, N_MLP, N_REQ)
    r_idx = jnp.arange(N_REQ, dtype=jnp.int32)[:, None, None]
    m_idx = jnp.arange(N_MLP, dtype=jnp.int32)[None, :, None]
    slot = serve_slot.reshape(N_REQ, N_MLP, N_REQ)[holder, m_idx, r_idx]
    flat = ((holder * N_MLP + m_idx) * N_REQ + slot).astype(jnp.int32)
    fetched = page_pool[flat].reshape(N_REQ, N_MLP, rows, 2 * HD)

    def one(items):
        q_r, n_r, p_r, t_r, f_r, pl_r, tl_r = items
        first = attend(q_r[0], n_r[0], p_r, t_r, pl_r[0], tl_r[0])
        q_b = q_r[1].reshape(N_MLP, samp_dev, 2, H * HD)
        n_b = n_r[1].reshape(N_MLP, samp_dev, 2, 2 * HD)
        tl_b = tl_r[1].reshape(N_MLP, samp_dev)
        wins = f_r[:, :WIN]
        tls = f_r[:, WIN:].reshape(N_MLP, samp_dev, TAIL, 2 * HD)
        second = jax.vmap(attend, in_axes=(0, 0, 0, 0, None, 0))(q_b, n_b, wins, tls, pl_r[1], tl_b)
        second = second.reshape(SAMPLES, 2, H * HD)
        tails_a = extend(t_r, n_r[0], tl_r[0])
        tails_b = extend(tls.reshape(SAMPLES, TAIL, 2 * HD), n_r[1], tl_r[1])
        return (jnp.stack([first, second]), jnp.stack([tails_a, tails_b]))
    attn, tails_out = lax.map(one, (queries, new_kv, prompt_kv, tail_kv, fetched, prompt_len, tail_len))
    mixed = jnp.dot(attn.reshape(-1, H * HD), w_out, preferred_element_type=jnp.float32)
    h1 = (residual.reshape(-1, D).astype(jnp.float32) + mixed).astype(jnp.bfloat16)
    normed = (rms_scale(h1.astype(jnp.float32)) * norm_mlp).astype(jnp.bfloat16)
    gate = jnp.dot(normed, w_gate, preferred_element_type=jnp.float32)
    up = jnp.dot(normed, w_up, preferred_element_type=jnp.float32)
    act = (jax.nn.gelu(gate, approximate=True) * up).astype(jnp.bfloat16)
    h2 = h1.astype(jnp.float32) + jnp.dot(act, w_down, preferred_element_type=jnp.float32)
    scores = lax.optimization_barrier(jnp.sum(rms_scale(h2) * norm_final * w_score, axis=-1))
    return (scores.reshape(N_REQ, 2, SAMPLES, 2), h2.astype(jnp.bfloat16).reshape(N_REQ, 2, SAMPLES, 2, D), tails_out)
```

```python
import functools

import jax
import jax.numpy as jnp
from jax import lax
from jax.experimental import pallas as pl
from jax.experimental.pallas import tpu as pltpu
from jax.sharding import PartitionSpec as P

BF = jnp.bfloat16
F32 = jnp.float32
NEG = -1e30
VMEM = pl.BlockSpec(memory_space=pltpu.VMEM)
SMEM = pl.BlockSpec(memory_space=pltpu.SMEM)
HBM = pl.BlockSpec(memory_space=pltpu.HBM)


def call(body, outs, operands, specs, scratch=(), flops=0, nbytes=0, limit=8):
    return pl.pallas_call(
        body,
        out_shape=outs,
        in_specs=specs,
        out_specs=jax.tree.map(lambda _: VMEM, outs),
        scratch_shapes=scratch,
        cost_estimate=pl.CostEstimate(flops=flops, bytes_accessed=nbytes, transcendentals=0),
        compiler_params=pltpu.CompilerParams(vmem_limit_bytes=limit << 20),
    )(*operands)


def iota(shape, axis):
    return lax.broadcasted_iota(jnp.int32, shape, axis)


def pick_pages(pool_ref, slot_ref, out_ref, scr):
    rows, slots, width = pool_ref.shape
    dests = slot_ref.shape[1]
    half = width // 2
    hot = (iota((slots, dests), 0) == slot_ref[...]).astype(F32).T.astype(BF)
    for i in range(rows):
        got = jnp.dot(hot, pool_ref[i], preferred_element_type=F32)
        scr[pl.ds(i, dests, stride=2 * rows), :] = got[:, :half]
        scr[pl.ds(rows + i, dests, stride=2 * rows), :] = got[:, half:]
    out_ref[...] = scr[...].astype(BF)


def load_rows(ref, q, lanes=None):
    parts = [ref[0, q, s].astype(F32) for s in range(ref.shape[2])]
    return jnp.concatenate(parts, axis=0)


def stack_heads(q8, size):
    heads = q8.shape[1] // size
    parts = [q8[:, h * size : (h + 1) * size] for h in range(heads)]
    return jnp.concatenate(parts, axis=0).astype(BF)


def row_lengths(tlen_ref, q, count):
    r = iota((2 * count, 1), 0)
    sample, token = r >> 1, r & 1
    length = jnp.zeros((2 * count, 1), jnp.int32)
    for s in range(count):
        length = jnp.where(sample == s, tlen_ref[0, q, s], length)
    return sample, token, length


def to_bias(visible):
    return jnp.where(visible, 0.0, NEG).astype(F32)


def window_bias(pos, plen, win, tail, sample, token, length):
    back = pos - win
    in_win = (pos < win) & (pos >= win - plen) & (pos > length + token)
    first = sample * tail
    in_tail = (back >= first) & (back < first + length)
    return to_bias(in_win | in_tail)


def new_bias(sample, token, count):
    c = iota((1, 2 * count), 1)
    return to_bias(((c >> 1) == sample) & ((c & 1) <= token))


def attend(qh, segments, rows, size):
    scale = 1.0 / jnp.sqrt(F32(size))
    heads = qh.shape[0] // rows
    scored = []
    top = None
    for keys, _, bias, _ in segments:
        s = lax.dot_general(qh, keys, (((1,), (1,)), ((), ())), preferred_element_type=F32)
        n = s.shape[1]
        s = s.reshape(heads, rows, n) * scale + bias[None]
        s = s.reshape(heads * rows, n)
        scored.append(s)
        m = s.max(axis=1, keepdims=True)
        top = m if top is None else jnp.maximum(top, m)
    total = None
    acc = None
    for s, (_, values, _, shift) in zip(scored, segments):
        e = jnp.exp(s - top)
        t = e.sum(axis=1, keepdims=True)
        if shift:
            e = pltpu.roll(e, shift, axis=1)
        o = jnp.dot(e.astype(BF), values, preferred_element_type=F32)
        total = t if total is None else total + t
        acc = o if acc is None else acc + o
    acc = acc / total
    return jnp.concatenate([acc[h * rows : (h + 1) * rows] for h in range(heads)], axis=1)


def resident(win, tail, size, page, q_ref, new_ref, kv_ref, tails_ref, holder_ref, plen_ref, tlen_ref, out_ref, bias_ref):
    count = q_ref.shape[2]
    rows = 2 * count
    sample, token, length = row_lengths(tlen_ref, 0, count)
    q8 = load_rows(q_ref, 0)
    qh = stack_heads(q8, size)
    fresh = load_rows(new_ref, 0).astype(BF)
    tails = tails_ref[0].reshape(count * tail, 2 * size)
    window = kv_ref[0]
    wb = window_bias(iota((1, win), 1), plen_ref[0, 0], win, tail, sample, token, length)
    tb = window_bias(win + iota((1, count * tail), 1), plen_ref[0, 0], win, tail, sample, token, length)
    nb = new_bias(sample, token, count)
    out = attend(
        qh,
        [
            (window[:, :size], window[:, size:], wb, 0),
            (tails[:, :size], tails[:, size:], tb, 0),
            (fresh[:, :size], fresh[:, size:], nb, 0),
        ],
        rows,
        size,
    )
    out_ref[...] = out.astype(BF)
    n = bias_ref.shape[1]
    c = iota((1, n), 1)
    pages = holder_ref.shape[1]
    per = n // pages
    origin = (c * (-(-(1 << 21) // per))) >> 21
    inside = c - origin * per
    base = jnp.zeros((1, n), jnp.int32)
    for p in range(pages):
        base = jnp.where(origin == holder_ref[0, p], p * page, base)
    pos = jnp.where(inside < page, base + inside, 1 << 20)
    sample, token, length = row_lengths(tlen_ref, 1, count)
    bias_ref[...] = window_bias(pos, plen_ref[0, 1], win, tail, sample, token, length)


def moved(size, page, where_ref, q_ref, new_ref, arr_ref, bias_ref, first_ref, res_ref, norm_ref, own_hbm, a1, a2, a3, b1, b2, b3, h1_ref, normed_ref, wown, attn, sem):
    fetch = pltpu.make_async_copy(own_hbm, wown, sem)
    fetch.start()
    wa, wb = (a1, a2, a3), (b1, b2, b3)
    count = q_ref.shape[2]
    rows = 2 * count
    r = iota((rows, 1), 0)
    qh = stack_heads(load_rows(q_ref, 1), size)
    fresh = load_rows(new_ref, 1).astype(BF)
    nb = new_bias(r >> 1, r & 1, count)
    arr = arr_ref[...]
    second = attend(
        qh,
        [(arr, arr, bias_ref[...], page), (fresh[:, :size], fresh[:, size:], nb, 0)],
        rows,
        size,
    )
    attn[...] = jnp.concatenate([first_ref[...].astype(F32), second], axis=0).astype(BF)
    me, core = where_ref[0, 0], where_ref[0, 1]
    block = wown.shape[0]
    n_mlp = len(wa) + 1

    def piece(k):
        rb = lax.rem(me - k + n_mlp, n_mlp)
        return attn[:, pl.ds(pl.multiple_of(rb * block, 128), block)]

    same = other = None
    for k in range(1, n_mlp):
        x = piece(k)
        s = jnp.dot(x, wa[k - 1][...], preferred_element_type=F32)
        o = jnp.dot(x, wb[k - 1][...], preferred_element_type=F32)
        same = s if same is None else same + s
        other = o if other is None else other + o
    fetch.wait()
    own = jnp.dot(piece(0), wown[...], preferred_element_type=F32)
    low = core == 0
    left = jnp.where(low, same, other)
    right = jnp.where(low, other, same)
    mixed = own + jnp.concatenate([left, right], axis=1)
    res = jnp.concatenate([load_rows(res_ref, 0), load_rows(res_ref, 1)], axis=0)
    h1 = (res + mixed).astype(BF)
    h1_ref[...] = h1
    f = h1.astype(F32)
    inv = lax.rsqrt(jnp.mean(f * f, axis=1, keepdims=True) + 1e-6)
    normed_ref[...] = (f * inv * norm_ref[...]).astype(BF)


def write_tails(win, page, arr_ref, tails_ref, new_ref, holder_ref, tlen_ref, out_ref, scr):
    count, tail, width = tails_ref.shape[1:]
    half = width // 2
    pages = holder_ref.shape[1]
    start = win // page
    lead = win - start * page
    for p in range(start, pages):
        block = arr_ref[holder_ref[0, p]].astype(F32)
        off = (p - start) * page
        scr[off : off + page, :half] = block[:page]
        scr[off : off + page, half:] = block[page:]
    row = iota((tail, 1), 0)
    for q in range(2):
        for s in range(count):
            if q == 0:
                old = tails_ref[0, s].astype(F32)
            else:
                old = scr[lead + s * tail : lead + (s + 1) * tail, :]
            fresh = new_ref[0, q, s].astype(F32)
            length = tlen_ref[0, q, s]
            t = jnp.where(row == length, fresh[0:1], old)
            t = jnp.where(row == length + 1, fresh[1:2], t)
            out_ref[0, q, s] = t.astype(BF)


def mlp(x0, x1, x2, x3, wg_hbm, wu_hbm, wd_hbm, y0, y1, y2, y3, wg, wu, wd, sems):
    cuts = 3
    kin, kout = wg.shape[0] // cuts, wd.shape[0] // cuts
    ups, downs = [], []
    for c in range(cuts):
        at = pl.ds(c * kin, kin)
        ups.append(
            (
                pltpu.make_async_copy(wg_hbm.at[at], wg.at[at], sems.at[3 * c]),
                pltpu.make_async_copy(wu_hbm.at[at], wu.at[at], sems.at[3 * c + 1]),
            )
        )
        at = pl.ds(c * kout, kout)
        downs.append(pltpu.make_async_copy(wd_hbm.at[at], wd.at[at], sems.at[3 * c + 2]))
    for g, u in ups:
        g.start()
        u.start()
    for d in downs:
        d.start()
    x = jnp.concatenate([x0[...], x1[...], x2[...], x3[...]], axis=0)
    gate = up = None
    for c, (g, u) in enumerate(ups):
        part = x[:, c * kin : (c + 1) * kin]
        g.wait()
        t = jnp.dot(part, wg[c * kin : (c + 1) * kin], preferred_element_type=F32)
        gate = t if gate is None else gate + t
        u.wait()
        t = jnp.dot(part, wu[c * kin : (c + 1) * kin], preferred_element_type=F32)
        up = t if up is None else up + t
    act = (jax.nn.gelu(gate, approximate=True) * up).astype(BF)
    y = None
    for c, d in enumerate(downs):
        d.wait()
        t = jnp.dot(act[:, c * kout : (c + 1) * kout], wd[c * kout : (c + 1) * kout], preferred_element_type=F32)
        y = t if y is None else y + t
    n = x0.shape[0]
    y0[...] = y[:n]
    y1[...] = y[n : 2 * n].astype(BF)
    y2[...] = y[2 * n : 3 * n].astype(BF)
    y3[...] = y[3 * n :].astype(BF)


def finish(h1_ref, y0, y1, y2, y3, nf_ref, ws_ref, score_ref, hid_ref):
    h2 = h1_ref[...].astype(F32) + (y0[...] + y1[...].astype(F32) + y2[...].astype(F32) + y3[...].astype(F32))
    inv = lax.rsqrt(jnp.mean(h2 * h2, axis=1, keepdims=True) + 1e-6)
    sc = jnp.sum(h2 * inv * nf_ref[...] * ws_ref[...], axis=1, keepdims=True)
    n = h2.shape[0]
    count = n // 4
    row, col = iota((n, count), 0), iota((n, count), 1)
    for q in range(2):
        for t in range(2):
            hit = row == q * 2 * count + col * 2 + t
            score_ref[0, q, t : t + 1, :] = jnp.sum(jnp.where(hit, sc, 0.0), axis=0, keepdims=True)
        for s in range(count):
            r = q * 2 * count + s * 2
            hid_ref[0, q, s] = h2[r : r + 2].astype(BF)


def on_device(
    n_req,
    n_mlp,
    queries,
    new_kv,
    residual,
    prompt_kv,
    tail_kv,
    page_pool,
    page_holder,
    serve_slot,
    prompt_len,
    tail_len,
    w_out,
    norm_mlp,
    w_gate,
    w_up,
    w_down,
    norm_final,
    w_score,
):
    samp, width = residual.shape[2], residual.shape[-1]
    size = new_kv.shape[-1] // 2
    win, tail = prompt_kv.shape[1], tail_kv.shape[2]
    slots, page = page_pool.shape[:2]
    rows = 4 * samp
    me = lax.axis_index("mlp")
    core = lax.rem(lax.axis_index("req"), 2)
    place = jnp.stack([me, core]).astype(jnp.int32)[None]
    arrived_rows = n_req * 2 * page

    def shift(x, k):
        return lax.ppermute(x, "mlp", [(i, (i + k) % n_mlp) for i in range(n_mlp)])

    half = width // 2
    mine = lax.dynamic_slice_in_dim(w_out, core * half, half, 1)
    slot, mine = lax.optimization_barrier((serve_slot, mine))
    same = [shift(mine, k) for k in range(1, n_mlp)]

    outgoing = call(
        pick_pages,
        jax.ShapeDtypeStruct((arrived_rows, size), BF),
        (jnp.transpose(page_pool, (1, 0, 2)), slot),
        [VMEM, VMEM],
        [pltpu.VMEM((arrived_rows, size), F32)],
        flops=100_000_000,
        nbytes=1_400_000,
    )
    arrived = lax.all_to_all(
        outgoing.reshape(n_req, 2 * page, size), "req", split_axis=0, concat_axis=0, tiled=True
    )
    q_late, outgoing = lax.optimization_barrier((queries, outgoing))
    first, bias = call(
        functools.partial(resident, win, tail, size, page),
        (jax.ShapeDtypeStruct((2 * samp, width), BF), jax.ShapeDtypeStruct((2 * samp, arrived_rows), F32)),
        (q_late, new_kv, prompt_kv, tail_kv, page_holder, prompt_len, tail_len),
        [VMEM, VMEM, VMEM, VMEM, SMEM, SMEM, SMEM],
        flops=100_000_000,
        nbytes=1_000_000,
    )
    *same, first = lax.optimization_barrier((*same, first))
    other = [lax.ppermute(a, "req", [(i, i ^ 1) for i in range(n_req)]) for a in same]
    tails_out = call(
        functools.partial(write_tails, win, page),
        jax.ShapeDtypeStruct((1, 2) + tail_kv.shape[1:], BF),
        (arrived, tail_kv, new_kv, page_holder, tail_len),
        [VMEM, VMEM, VMEM, SMEM, SMEM],
        [pltpu.VMEM(((n_req - win // page) * page, 2 * size), F32)],
        flops=1_000_000,
        nbytes=1_500_000,
    )
    block = w_out.shape[0]
    h1, normed = call(
        functools.partial(moved, size, page),
        (jax.ShapeDtypeStruct((rows, width), BF), jax.ShapeDtypeStruct((rows, width), BF)),
        (
            place,
            queries,
            new_kv,
            arrived.reshape(arrived_rows, size),
            bias,
            first,
            residual,
            norm_mlp[None],
            w_out,
            *same,
            *other,
        ),
        [SMEM] + [VMEM] * 7 + [HBM] + [VMEM] * 6,
        [
            pltpu.VMEM((block, width), BF),
            pltpu.VMEM((rows, width), BF),
            pltpu.SemaphoreType.DMA,
        ],
        limit=14,
        flops=200_000_000,
        nbytes=6_000_000,
    )
    others = [shift(normed, k) for k in range(1, n_mlp)]
    row_bf = jax.ShapeDtypeStruct((rows, width), BF)
    hid = w_gate.shape[1]
    ys = call(
        mlp,
        (jax.ShapeDtypeStruct((rows, width), F32), row_bf, row_bf, row_bf),
        (normed, *others, w_gate, w_up, w_down),
        [VMEM] * 4 + [HBM] * 3,
        [
            pltpu.VMEM((width, hid), BF),
            pltpu.VMEM((width, hid), BF),
            pltpu.VMEM((hid, width), BF),
            pltpu.SemaphoreType.DMA((9,)),
        ],
        flops=700_000_000,
        nbytes=11_000_000,
        limit=16,
    )
    back = [shift(ys[k], -k) for k in range(1, n_mlp)]
    scores, hidden = call(
        finish,
        (jax.ShapeDtypeStruct((1, 2, 2, samp), F32), jax.ShapeDtypeStruct(residual.shape, BF)),
        (h1, ys[0], *back, norm_final[None], w_score[None]),
        [VMEM] * 7,
        flops=1_000_000,
        nbytes=500_000,
    )
    return (jnp.transpose(scores, (0, 1, 3, 2)), hidden, tails_out)


def solution(mesh):
    placed = (
        P("req", None, "mlp", None, None),
        P("req", None, "mlp", None, None),
        P("req", None, "mlp", None, None),
        P("req", None, None),
        P("req", "mlp", None, None),
        P(("req", "mlp"), None, None),
        P(("req", "mlp"), None),
        P(("req", "mlp"), None),
        P("req", None),
        P("req", None, "mlp"),
        P("mlp", None),
        P(),
        P(None, "mlp"),
        P(None, "mlp"),
        P("mlp", None),
        P(),
        P(),
    )
    return jax.shard_map(
        functools.partial(on_device, mesh.shape["req"], mesh.shape["mlp"]),
        mesh=mesh,
        in_specs=placed,
        out_specs=(
            P("req", None, "mlp", None),
            P("req", None, "mlp", None, None),
            P("req", None, "mlp", None, None),
        ),
        check_vma=False,
    )
```

```python
import functools

import jax
import jax.numpy as jnp
from jax import lax
from jax.experimental import pallas as pl
from jax.experimental.pallas import tpu as pltpu
from jax.sharding import PartitionSpec as P

BF = jnp.bfloat16
F32 = jnp.float32
NEG = -1e30
VMEM = pl.BlockSpec(memory_space=pltpu.VMEM)
SMEM = pl.BlockSpec(memory_space=pltpu.SMEM)
HBM = pl.BlockSpec(memory_space=pltpu.HBM)


def call(body, outs, operands, specs, scratch=(), flops=0, nbytes=0, limit=8):
    return pl.pallas_call(
        body,
        out_shape=outs,
        in_specs=specs,
        out_specs=jax.tree.map(lambda _: VMEM, outs),
        scratch_shapes=scratch,
        cost_estimate=pl.CostEstimate(flops=flops, bytes_accessed=nbytes, transcendentals=0),
        compiler_params=pltpu.CompilerParams(vmem_limit_bytes=limit << 20),
    )(*operands)


def iota(shape, axis):
    return lax.broadcasted_iota(jnp.int32, shape, axis)


def pick_pages(pool_ref, slot_ref, out_ref, scr):
    rows, slots, width = pool_ref.shape
    dests = slot_ref.shape[1]
    half = width // 2
    hot = (iota((slots, dests), 0) == slot_ref[...]).astype(F32).T.astype(BF)
    for i in range(rows):
        got = jnp.dot(hot, pool_ref[i], preferred_element_type=F32)
        scr[pl.ds(i, dests, stride=2 * rows), :] = got[:, :half]
        scr[pl.ds(rows + i, dests, stride=2 * rows), :] = got[:, half:]
    out_ref[...] = scr[...].astype(BF)


def take_half(w_hbm, out_ref, sem):
    half = out_ref.shape[1]
    core = lax.rem(lax.axis_index("req"), 2)
    copy = pltpu.make_async_copy(w_hbm.at[:, pl.ds(pl.multiple_of(core * half, 128), half)], out_ref, sem)
    copy.start()
    copy.wait()


def load_rows(ref, q):
    parts = [ref[0, q, s].astype(F32) for s in range(ref.shape[2])]
    return jnp.concatenate(parts, axis=0)


def stack_heads(q8, size):
    heads = q8.shape[1] // size
    parts = [q8[:, h * size : (h + 1) * size] for h in range(heads)]
    return jnp.concatenate(parts, axis=0).astype(BF)


def row_lengths(tlen_ref, q, count):
    r = iota((2 * count, 1), 0)
    sample, token = r >> 1, r & 1
    length = jnp.zeros((2 * count, 1), jnp.int32)
    for s in range(count):
        length = jnp.where(sample == s, tlen_ref[0, q, s], length)
    return sample, token, length


def to_bias(visible):
    return jnp.where(visible, 0.0, NEG).astype(F32)


def window_bias(pos, plen, win, tail, sample, token, length):
    back = pos - win
    in_win = (pos < win) & (pos >= win - plen) & (pos > length + token)
    first = sample * tail
    in_tail = (back >= first) & (back < first + length)
    return to_bias(in_win | in_tail)


def new_bias(sample, token, count):
    c = iota((1, 2 * count), 1)
    return to_bias(((c >> 1) == sample) & ((c & 1) <= token))


def attend(qh, segments, rows, size):
    scale = 1.0 / jnp.sqrt(F32(size))
    heads = qh.shape[0] // rows
    scored = []
    top = None
    for keys, _, bias, _ in segments:
        s = lax.dot_general(qh, keys, (((1,), (1,)), ((), ())), preferred_element_type=F32)
        n = s.shape[1]
        s = s.reshape(heads, rows, n) * scale + bias[None]
        s = s.reshape(heads * rows, n)
        scored.append(s)
        m = s.max(axis=1, keepdims=True)
        top = m if top is None else jnp.maximum(top, m)
    total = None
    acc = None
    for s, (_, values, _, shift) in zip(scored, segments):
        e = jnp.exp(s - top)
        t = e.sum(axis=1, keepdims=True)
        if shift:
            e = pltpu.roll(e, shift, axis=1)
        o = jnp.dot(e.astype(BF), values, preferred_element_type=F32)
        total = t if total is None else total + t
        acc = o if acc is None else acc + o
    acc = acc / total
    return jnp.concatenate([acc[h * rows : (h + 1) * rows] for h in range(heads)], axis=1)


def resident(win, tail, size, page, n, q_ref, new_ref, kv_ref, tails_ref, holder_ref, plen_ref, tlen_ref, res_ref, out_ref):
    count = q_ref.shape[2]
    rows = 2 * count
    sample, token, length = row_lengths(tlen_ref, 0, count)
    q8 = load_rows(q_ref, 0)
    qh = stack_heads(q8, size)
    fresh = load_rows(new_ref, 0).astype(BF)
    tails = tails_ref[0].reshape(count * tail, 2 * size)
    window = kv_ref[0]
    wb = window_bias(iota((1, win), 1), plen_ref[0, 0], win, tail, sample, token, length)
    tb = window_bias(win + iota((1, count * tail), 1), plen_ref[0, 0], win, tail, sample, token, length)
    nb = new_bias(sample, token, count)
    out = attend(
        qh,
        [
            (window[:, :size], window[:, size:], wb, 0),
            (tails[:, :size], tails[:, size:], tb, 0),
            (fresh[:, :size], fresh[:, size:], nb, 0),
        ],
        rows,
        size,
    )
    c = iota((1, n), 1)
    pages = holder_ref.shape[1]
    per = n // pages
    origin = (c * (-(-(1 << 21) // per))) >> 21
    inside = c - origin * per
    base = jnp.zeros((1, n), jnp.int32)
    for p in range(pages):
        base = jnp.where(origin == holder_ref[0, p], p * page, base)
    pos = jnp.where(inside < page, base + inside, 1 << 20)
    sample, token, length = row_lengths(tlen_ref, 1, count)
    bias = window_bias(pos, plen_ref[0, 1], win, tail, sample, token, length)
    parts = (bias, load_rows(res_ref, 0), load_rows(res_ref, 1), out, load_rows(q_ref, 1), load_rows(new_ref, 1))
    out_ref[...] = jnp.concatenate(parts, axis=1)


def moved(size, page, arr_ref, norm_ref, *refs):
    count = len(refs) // 2 - 2
    hbm, (h1_ref, normed_ref), vmem, (attn, sems) = refs[:count], refs[count : count + 2], refs[count + 2 : -2], refs[-2:]
    copies = [pltpu.make_async_copy(a, b, sems.at[i]) for i, (a, b) in enumerate(zip(hbm, vmem))]
    for c in copies:
        c.start()
    state, wown, a1, a3, top, bot, b13, btop, bbot = vmem
    copies[0].wait()
    n, width = arr_ref.shape[0], attn.shape[1]
    at = [n + i * width for i in range(5)]
    bias = state[:, :n]
    res = jnp.concatenate([state[:, at[0] : at[1]], state[:, at[1] : at[2]]], axis=0)
    first, q8, fresh = state[:, at[2] : at[3]], state[:, at[3] : at[4]], state[:, at[4] :].astype(BF)
    rows = state.shape[0]
    r = iota((rows, 1), 0)
    nb = new_bias(r >> 1, r & 1, rows // 2)
    arr = arr_ref[...]
    second = attend(
        stack_heads(q8, size),
        [(arr, arr, bias, page), (fresh[:, :size], fresh[:, size:], nb, 0)],
        rows,
        size,
    )
    attn[...] = jnp.concatenate([first, second], axis=0).astype(BF)
    for c in copies[1:]:
        c.wait()
    me = lax.axis_index("mlp")
    low = lax.rem(lax.axis_index("req"), 2) == 0
    block = wown.shape[0]
    n_mlp = attn.shape[1] // block
    part = top.shape[0]

    def piece(k, first=0, count=block):
        rb = lax.rem(me - k + n_mlp, n_mlp)
        return attn[:, pl.ds(pl.multiple_of(rb * block, 128), block)][:, first : first + count]

    def product(x, w):
        return jnp.dot(x, w[...], preferred_element_type=F32)

    p1, p3, pt, pb = piece(1), piece(n_mlp - 1), piece(2, 0, part), piece(2, part, block - part)
    same = product(p1, a1) + product(p3, a3) + product(pt, top) + product(pb, bot)
    other = product(p1, b13.at[0]) + product(p3, b13.at[1]) + product(pt, btop) + product(pb, bbot)
    own = product(piece(0), wown)
    left = jnp.where(low, same, other)
    right = jnp.where(low, other, same)
    mixed = own + jnp.concatenate([left, right], axis=1)
    h1 = (res + mixed).astype(BF)
    h1_ref[...] = h1
    f = h1.astype(F32)
    inv = lax.rsqrt(jnp.mean(f * f, axis=1, keepdims=True) + 1e-6)
    normed_ref[...] = (f * inv * norm_ref[...]).astype(BF)


def write_tails(win, page, arr_ref, tails_ref, new_ref, holder_ref, tlen_ref, out_ref, scr):
    count, tail, width = tails_ref.shape[1:]
    half = width // 2
    pages = holder_ref.shape[1]
    start = win // page
    lead = win - start * page
    for p in range(start, pages):
        block = arr_ref[holder_ref[0, p]].astype(F32)
        off = (p - start) * page
        scr[off : off + page, :half] = block[:page]
        scr[off : off + page, half:] = block[page:]
    row = iota((tail, 1), 0)
    for q in range(2):
        for s in range(count):
            if q == 0:
                old = tails_ref[0, s].astype(F32)
            else:
                old = scr[lead + s * tail : lead + (s + 1) * tail, :]
            fresh = new_ref[0, q, s].astype(F32)
            length = tlen_ref[0, q, s]
            t = jnp.where(row == length, fresh[0:1], old)
            t = jnp.where(row == length + 1, fresh[1:2], t)
            out_ref[0, q, s] = t.astype(BF)


def load(*refs):
    count = len(refs) // 2
    sems = refs[-1]
    copies = [pltpu.make_async_copy(refs[i], refs[count + i], sems.at[i]) for i in range(count)]
    for c in copies:
        c.start()
    for c in copies:
        c.wait()


def mlp(x0, x1, x2, x3, wg, wu, wd, y0, y1, y2, y3):
    x = jnp.concatenate([x0[...], x1[...], x2[...], x3[...]], axis=0)
    gate = jnp.dot(x, wg[...], preferred_element_type=F32)
    up = jnp.dot(x, wu[...], preferred_element_type=F32)
    act = (jax.nn.gelu(gate, approximate=True) * up).astype(BF)
    y = jnp.dot(act, wd[...], preferred_element_type=F32)
    n = x0.shape[0]
    y0[...] = y[:n]
    y1[...] = y[n : 2 * n].astype(BF)
    y2[...] = y[2 * n : 3 * n].astype(BF)
    y3[...] = y[3 * n :].astype(BF)


def finish(h1_ref, y0, y1, y2, y3, nf_ref, ws_ref, score_ref, hid_ref):
    h2 = h1_ref[...].astype(F32) + (y0[...] + y1[...].astype(F32) + y2[...].astype(F32) + y3[...].astype(F32))
    inv = lax.rsqrt(jnp.mean(h2 * h2, axis=1, keepdims=True) + 1e-6)
    sc = jnp.sum(h2 * inv * nf_ref[...] * ws_ref[...], axis=1, keepdims=True)
    n = h2.shape[0]
    count = n // 4
    row, col = iota((n, count), 0), iota((n, count), 1)
    for q in range(2):
        for t in range(2):
            hit = row == q * 2 * count + col * 2 + t
            score_ref[0, q, t : t + 1, :] = jnp.sum(jnp.where(hit, sc, 0.0), axis=0, keepdims=True)
        for s in range(count):
            r = q * 2 * count + s * 2
            hid_ref[0, q, s] = h2[r : r + 2].astype(BF)


def on_device(
    n_req,
    n_mlp,
    queries,
    new_kv,
    residual,
    prompt_kv,
    tail_kv,
    page_pool,
    page_holder,
    serve_slot,
    prompt_len,
    tail_len,
    w_out,
    norm_mlp,
    w_gate,
    w_up,
    w_down,
    norm_final,
    w_score,
):
    samp, width = residual.shape[2], residual.shape[-1]
    size = new_kv.shape[-1] // 2
    win, tail = prompt_kv.shape[1], tail_kv.shape[2]
    slots, page = page_pool.shape[:2]
    rows = 4 * samp
    arrived_rows = n_req * 2 * page
    block, hid = w_out.shape[0], w_gate.shape[1]
    half, part = width // 2, block // 2

    def shift(x, k):
        return lax.ppermute(x, "mlp", [(i, (i + k) % n_mlp) for i in range(n_mlp)])

    def swap(x):
        return lax.ppermute(x, "req", [(i, i ^ 1) for i in range(n_req)])

    mine = call(
        take_half,
        jax.ShapeDtypeStruct((block, half), BF),
        (w_out,),
        [HBM],
        [pltpu.SemaphoreType.DMA],
        nbytes=1_200_000,
        limit=60,
    )
    a1, a3 = shift(mine, 1), shift(mine, -1)
    slot, _ = lax.optimization_barrier((serve_slot, mine))
    outgoing = call(
        pick_pages,
        jax.ShapeDtypeStruct((arrived_rows, size), BF),
        (jnp.transpose(page_pool, (1, 0, 2)), slot),
        [VMEM, VMEM],
        [pltpu.VMEM((arrived_rows, size), F32)],
        flops=100_000_000,
        nbytes=1_400_000,
        limit=60,
    )
    arrived = lax.all_to_all(
        outgoing.reshape(n_req, 2 * page, size), "req", split_axis=0, concat_axis=0, tiled=True
    )
    q_late, outgoing = lax.optimization_barrier((queries, outgoing))
    span = arrived_rows + 4 * width + 2 * size
    state = call(
        functools.partial(resident, win, tail, size, page, arrived_rows),
        jax.ShapeDtypeStruct((2 * samp, span), F32),
        (q_late, new_kv, prompt_kv, tail_kv, page_holder, prompt_len, tail_len, residual),
        [VMEM, VMEM, VMEM, VMEM, SMEM, SMEM, SMEM, VMEM],
        flops=100_000_000,
        nbytes=1_000_000,
        limit=60,
    )
    a1, a3, state = lax.optimization_barrier((a1, a3, state))
    top, bot = shift(a1[:part], 1), shift(a3[part:], -1)
    b13, btop, bbot = swap(jnp.stack([a1, a3])), swap(top), swap(bot)
    tails_out = call(
        functools.partial(write_tails, win, page),
        jax.ShapeDtypeStruct((1, 2) + tail_kv.shape[1:], BF),
        (arrived, tail_kv, new_kv, page_holder, tail_len),
        [VMEM, VMEM, VMEM, SMEM, SMEM],
        [pltpu.VMEM(((n_req - win // page) * page, 2 * size), F32)],
        flops=1_000_000,
        nbytes=1_500_000,
    )
    pieces = (state, w_out, a1, a3, top, bot, b13, btop, bbot)
    row_bf = jax.ShapeDtypeStruct((rows, width), BF)
    h1, normed = call(
        functools.partial(moved, size, page),
        (row_bf, row_bf),
        (arrived.reshape(arrived_rows, size), norm_mlp[None], *pieces),
        [VMEM, VMEM] + [HBM] * len(pieces),
        [pltpu.VMEM(x.shape, x.dtype) for x in pieces]
        + [pltpu.VMEM((rows, width), BF), pltpu.SemaphoreType.DMA((len(pieces),))],
        flops=200_000_000,
        nbytes=6_000_000,
        limit=50,
    )
    others = [shift(normed, k) for k in range(1, n_mlp)]
    w_up, w_down, _ = lax.optimization_barrier((w_up, w_down, normed))
    w_up, w_down = call(
        load,
        (pltpu.VMEM(w_up.shape, BF), pltpu.VMEM(w_down.shape, BF)),
        (w_up, w_down),
        [HBM, HBM],
        [pltpu.SemaphoreType.DMA((2,))],
        nbytes=14_000_000,
        limit=50,
    )
    ys = call(
        mlp,
        (jax.ShapeDtypeStruct((rows, width), F32), row_bf, row_bf, row_bf),
        (normed, *others, w_gate, w_up, w_down),
        [VMEM] * 7,
        flops=700_000_000,
        nbytes=1_000_000,
        limit=14,
    )
    back = [shift(ys[k], -k) for k in range(1, n_mlp)]
    scores, hidden = call(
        finish,
        (jax.ShapeDtypeStruct((1, 2, 2, samp), F32), jax.ShapeDtypeStruct(residual.shape, BF)),
        (h1, ys[0], *back, norm_final[None], w_score[None]),
        [VMEM] * 7,
        flops=1_000_000,
        nbytes=500_000,
    )
    return (jnp.transpose(scores, (0, 1, 3, 2)), hidden, tails_out)


def solution(mesh):
    placed = (
        P("req", None, "mlp", None, None),
        P("req", None, "mlp", None, None),
        P("req", None, "mlp", None, None),
        P("req", None, None),
        P("req", "mlp", None, None),
        P(("req", "mlp"), None, None),
        P(("req", "mlp"), None),
        P(("req", "mlp"), None),
        P("req", None),
        P("req", None, "mlp"),
        P("mlp", None),
        P(),
        P(None, "mlp"),
        P(None, "mlp"),
        P("mlp", None),
        P(),
        P(),
    )
    return jax.shard_map(
        functools.partial(on_device, mesh.shape["req"], mesh.shape["mlp"]),
        mesh=mesh,
        in_specs=placed,
        out_specs=(
            P("req", None, "mlp", None),
            P("req", None, "mlp", None, None),
            P("req", None, "mlp", None, None),
        ),
        check_vma=False,
    )
```

```python
import functools

import jax
import jax.numpy as jnp
from jax import lax
from jax.experimental import pallas as pl
from jax.experimental.pallas import tpu as pltpu
from jax.sharding import PartitionSpec as P

BF = jnp.bfloat16
F32 = jnp.float32
NEG = -1e30
VMEM = pl.BlockSpec(memory_space=pltpu.VMEM)
SMEM = pl.BlockSpec(memory_space=pltpu.SMEM)
HBM = pl.BlockSpec(memory_space=pltpu.HBM)


def call(body, outs, operands, specs, scratch=(), flops=0, nbytes=0, limit=8, out_specs=None):
    return pl.pallas_call(
        body,
        out_shape=outs,
        in_specs=specs,
        out_specs=jax.tree.map(lambda _: VMEM, outs) if out_specs is None else out_specs,
        scratch_shapes=scratch,
        cost_estimate=pl.CostEstimate(flops=flops, bytes_accessed=nbytes, transcendentals=0),
        compiler_params=pltpu.CompilerParams(vmem_limit_bytes=limit << 20),
    )(*operands)


def iota(shape, axis):
    return lax.broadcasted_iota(jnp.int32, shape, axis)


def pick_pages(pool_ref, slot_ref, out_ref, scr):
    rows, slots, width = pool_ref.shape
    dests = slot_ref.shape[1]
    half = width // 2
    hot = (iota((slots, dests), 0) == slot_ref[...]).astype(F32).T.astype(BF)
    for i in range(rows):
        got = jnp.dot(hot, pool_ref[i], preferred_element_type=F32)
        scr[pl.ds(i, dests, stride=2 * rows), :] = got[:, :half]
        scr[pl.ds(rows + i, dests, stride=2 * rows), :] = got[:, half:]
    out_ref[...] = scr[...].astype(BF)


def load_rows(ref, q):
    parts = [ref[0, q, s].astype(F32) for s in range(ref.shape[2])]
    return jnp.concatenate(parts, axis=0)


def stack_heads(q8, size):
    heads = q8.shape[1] // size
    parts = [q8[:, h * size : (h + 1) * size] for h in range(heads)]
    return jnp.concatenate(parts, axis=0).astype(BF)


def row_lengths(tlen_ref, q, count):
    r = iota((2 * count, 1), 0)
    sample, token = r >> 1, r & 1
    length = jnp.zeros((2 * count, 1), jnp.int32)
    for s in range(count):
        length = jnp.where(sample == s, tlen_ref[0, q, s], length)
    return sample, token, length


def to_bias(visible):
    return jnp.where(visible, 0.0, NEG).astype(F32)


def window_bias(pos, plen, win, tail, sample, token, length):
    back = pos - win
    in_win = (pos < win) & (pos >= win - plen) & (pos > length + token)
    first = sample * tail
    in_tail = (back >= first) & (back < first + length)
    return to_bias(in_win | in_tail)


def new_bias(sample, token, count):
    c = iota((1, 2 * count), 1)
    return to_bias(((c >> 1) == sample) & ((c & 1) <= token))


def attend(qh, segments, rows, size):
    scale = 1.0 / jnp.sqrt(F32(size))
    heads = qh.shape[0] // rows
    scored = []
    top = None
    for keys, _, bias, _ in segments:
        s = lax.dot_general(qh, keys, (((1,), (1,)), ((), ())), preferred_element_type=F32)
        n = s.shape[1]
        s = s.reshape(heads, rows, n) * scale + bias[None]
        s = s.reshape(heads * rows, n)
        scored.append(s)
        m = s.max(axis=1, keepdims=True)
        top = m if top is None else jnp.maximum(top, m)
    total = None
    acc = None
    for s, (_, values, _, shift) in zip(scored, segments):
        e = jnp.exp(s - top)
        t = e.sum(axis=1, keepdims=True)
        if shift:
            e = pltpu.roll(e, shift, axis=1)
        o = jnp.dot(e.astype(BF), values, preferred_element_type=F32)
        total = t if total is None else total + t
        acc = o if acc is None else acc + o
    acc = acc / total
    return jnp.concatenate([acc[h * rows : (h + 1) * rows] for h in range(heads)], axis=1)


def resident(win, tail, size, page, n, q_ref, new_ref, kv_ref, tails_ref, holder_ref, plen_ref, tlen_ref, res_ref, out_ref):
    count = q_ref.shape[2]
    rows = 2 * count
    sample, token, length = row_lengths(tlen_ref, 0, count)
    q8 = load_rows(q_ref, 0)
    qh = stack_heads(q8, size)
    fresh = load_rows(new_ref, 0).astype(BF)
    tails = tails_ref[0].reshape(count * tail, 2 * size)
    window = kv_ref[0]
    wb = window_bias(iota((1, win), 1), plen_ref[0, 0], win, tail, sample, token, length)
    tb = window_bias(win + iota((1, count * tail), 1), plen_ref[0, 0], win, tail, sample, token, length)
    nb = new_bias(sample, token, count)
    out = attend(
        qh,
        [
            (window[:, :size], window[:, size:], wb, 0),
            (tails[:, :size], tails[:, size:], tb, 0),
            (fresh[:, :size], fresh[:, size:], nb, 0),
        ],
        rows,
        size,
    )
    c = iota((1, n), 1)
    pages = holder_ref.shape[1]
    per = n // pages
    origin = (c * (-(-(1 << 21) // per))) >> 21
    inside = c - origin * per
    base = jnp.zeros((1, n), jnp.int32)
    for p in range(pages):
        base = jnp.where(origin == holder_ref[0, p], p * page, base)
    pos = jnp.where(inside < page, base + inside, 1 << 20)
    sample, token, length = row_lengths(tlen_ref, 1, count)
    bias = window_bias(pos, plen_ref[0, 1], win, tail, sample, token, length)
    parts = (bias, load_rows(q_ref, 1), load_rows(new_ref, 1), load_rows(res_ref, 0), load_rows(res_ref, 1), out)
    out_ref[...] = jnp.concatenate(parts, axis=1).astype(BF)


def moved(size, page, arr_ref, state, norm_ref, *refs):
    count = len(refs) // 2 - 2
    hbm, (h1_ref, normed_ref), vmem, (attn, sems) = refs[:count], refs[count : count + 2], refs[count + 2 : -2], refs[-2:]
    copies = [pltpu.make_async_copy(a, b, sems.at[i]) for i, (a, b) in enumerate(zip(hbm, vmem))]
    for c in copies:
        c.start()
    wown, near, far, part_a, part_b = vmem
    n, width = arr_ref.shape[0], attn.shape[1]
    rows = state.shape[0]
    bias = state[:, :n].astype(F32)
    at = [n + width + 2 * size + i * width for i in range(4)]
    q8, fresh = state[:, n : n + width], state[:, n + width : at[0]]
    res = jnp.concatenate([state[:, at[0] : at[1]], state[:, at[1] : at[2]]], axis=0).astype(F32)
    first = state[:, at[2] : at[3]].astype(F32)
    r = iota((rows, 1), 0)
    nb = new_bias(r >> 1, r & 1, rows // 2)
    arr = arr_ref[...]
    second = attend(
        stack_heads(q8.astype(F32), size),
        [(arr, arr, bias, page), (fresh[:, :size], fresh[:, size:], nb, 0)],
        rows,
        size,
    )
    for c in copies:
        c.wait()
    attn[...] = jnp.concatenate([first, second], axis=0).astype(BF)
    me = lax.axis_index("mlp")
    core = lax.rem(lax.axis_index("req"), 2)
    block = wown.shape[0]
    n_mlp = width // block
    part = part_a.shape[0]

    def piece(k):
        rb = lax.rem(me + k + n_mlp, n_mlp)
        return attn[:, pl.ds(pl.multiple_of(rb * block, 128), block)]

    def product(x, w):
        return jnp.dot(x, w[...], preferred_element_type=F32)

    opposite = piece(2).astype(F32)
    low, high = opposite[:, :part], opposite[:, part:]
    mixed = product(piece(0), wown) + product(piece(2 * core - 1), near) + product(piece(1 - 2 * core), far)
    mixed = mixed + product(jnp.where(core == 0, low, high).astype(BF), part_a)
    mixed = mixed + product(jnp.where(core == 0, high, low).astype(BF), part_b)
    h1 = (res + mixed).astype(BF)
    h1_ref[...] = h1
    f = h1.astype(F32)
    inv = lax.rsqrt(jnp.mean(f * f, axis=1, keepdims=True) + 1e-6)
    normed_ref[...] = (f * inv * norm_ref[...]).astype(BF)


def write_tails(win, page, arr_ref, tails_ref, new_ref, holder_ref, tlen_ref, out_ref, scr):
    count, tail, width = tails_ref.shape[1:]
    half = width // 2
    pages = holder_ref.shape[1]
    start = win // page
    lead = win - start * page
    for p in range(start, pages):
        block = arr_ref[holder_ref[0, p]].astype(F32)
        off = (p - start) * page
        scr[off : off + page, :half] = block[:page]
        scr[off : off + page, half:] = block[page:]
    row = iota((tail, 1), 0)
    for q in range(2):
        for s in range(count):
            if q == 0:
                old = tails_ref[0, s].astype(F32)
            else:
                old = scr[lead + s * tail : lead + (s + 1) * tail, :]
            fresh = new_ref[0, q, s].astype(F32)
            length = tlen_ref[0, q, s]
            t = jnp.where(row == length, fresh[0:1], old)
            t = jnp.where(row == length + 1, fresh[1:2], t)
            out_ref[0, q, s] = t.astype(BF)


def load(*refs):
    count = len(refs) // 2
    sems = refs[-1]
    copies = [pltpu.make_async_copy(refs[i], refs[count + i], sems.at[i]) for i in range(count)]
    for c in copies:
        c.start()
    for c in copies:
        c.wait()


def mlp(x0, x1, x2, x3, wg, wu, wd, y0, y1, y2, y3):
    x = jnp.concatenate([x0[...], x1[...], x2[...], x3[...]], axis=0)
    gate = jnp.dot(x, wg[...], preferred_element_type=F32)
    up = jnp.dot(x, wu[...], preferred_element_type=F32)
    act = (jax.nn.gelu(gate, approximate=True) * up).astype(BF)
    y = jnp.dot(act, wd[...], preferred_element_type=F32)
    n = x0.shape[0]
    y0[...] = y[:n]
    y1[...] = y[n : 2 * n].astype(BF)
    y2[...] = y[2 * n : 3 * n].astype(BF)
    y3[...] = y[3 * n :].astype(BF)


def finish(h1_ref, y0, y1, y2, y3, nf_ref, ws_ref, score_ref, hid_ref):
    h2 = h1_ref[...].astype(F32) + (y0[...] + y1[...].astype(F32) + y2[...].astype(F32) + y3[...].astype(F32))
    inv = lax.rsqrt(jnp.mean(h2 * h2, axis=1, keepdims=True) + 1e-6)
    sc = jnp.sum(h2 * inv * nf_ref[...] * ws_ref[...], axis=1, keepdims=True)
    n = h2.shape[0]
    count = n // 4
    row, col = iota((n, count), 0), iota((n, count), 1)
    for q in range(2):
        for t in range(2):
            hit = row == q * 2 * count + col * 2 + t
            score_ref[0, q, t : t + 1, :] = jnp.sum(jnp.where(hit, sc, 0.0), axis=0, keepdims=True)
        for s in range(count):
            r = q * 2 * count + s * 2
            hid_ref[0, q, s] = h2[r : r + 2].astype(BF)


def on_device(
    n_req,
    n_mlp,
    queries,
    new_kv,
    residual,
    prompt_kv,
    tail_kv,
    page_pool,
    page_holder,
    serve_slot,
    prompt_len,
    tail_len,
    w_out,
    norm_mlp,
    w_gate,
    w_up,
    w_down,
    norm_final,
    w_score,
):
    samp, width = residual.shape[2], residual.shape[-1]
    size = new_kv.shape[-1] // 2
    win, tail = prompt_kv.shape[1], tail_kv.shape[2]
    slots, page = page_pool.shape[:2]
    rows = 4 * samp
    arrived_rows = n_req * 2 * page
    block, hid = w_out.shape[0], w_gate.shape[1]
    part = block // 2

    def shift(x, k):
        return lax.ppermute(x, "mlp", [(i, (i + k) % n_mlp) for i in range(n_mlp)])

    def swap(x):
        return lax.ppermute(x, "req", [(i, i ^ 1) for i in range(n_req)])

    def onward(x):
        to = [(r * n_mlp + m, r * n_mlp + (m + 1 - 2 * (r % 2)) % n_mlp) for r in range(n_req) for m in range(n_mlp)]
        return lax.ppermute(x, ("req", "mlp"), to)

    near = onward(w_out)
    outgoing = call(
        pick_pages,
        jax.ShapeDtypeStruct((arrived_rows, size), BF),
        (jnp.transpose(page_pool, (1, 0, 2)), serve_slot),
        [VMEM, VMEM],
        [pltpu.VMEM((arrived_rows, size), F32)],
        flops=100_000_000,
        nbytes=1_400_000,
        limit=60,
    )
    arrived = lax.all_to_all(
        outgoing.reshape(n_req, 2 * page, size), "req", split_axis=0, concat_axis=0, tiled=True
    )
    q_late, outgoing = lax.optimization_barrier((queries, outgoing))
    state = call(
        functools.partial(resident, win, tail, size, page, arrived_rows),
        jax.ShapeDtypeStruct((2 * samp, arrived_rows + 4 * width + 2 * size), BF),
        (q_late, new_kv, prompt_kv, tail_kv, page_holder, prompt_len, tail_len, residual),
        [VMEM, VMEM, VMEM, VMEM, SMEM, SMEM, SMEM, VMEM],
        flops=100_000_000,
        nbytes=1_000_000,
        limit=40,
    )
    core = lax.rem(lax.axis_index("req"), 2)
    part_a = onward(lax.dynamic_slice_in_dim(near, core * part, part, 0))
    far, part_b = swap(near), swap(part_a)
    tails_out = call(
        functools.partial(write_tails, win, page),
        jax.ShapeDtypeStruct((1, 2) + tail_kv.shape[1:], BF),
        (arrived, tail_kv, new_kv, page_holder, tail_len),
        [VMEM, VMEM, VMEM, SMEM, SMEM],
        [pltpu.VMEM(((n_req - win // page) * page, 2 * size), F32)],
        flops=1_000_000,
        nbytes=1_500_000,
    )
    pieces = (w_out, near, far, part_a, part_b)
    row_bf = jax.ShapeDtypeStruct((rows, width), BF)
    h1, normed = call(
        functools.partial(moved, size, page),
        (row_bf, row_bf),
        (arrived.reshape(arrived_rows, size), state, norm_mlp[None], *pieces),
        [VMEM] * 3 + [HBM] * len(pieces),
        [pltpu.VMEM(x.shape, x.dtype) for x in pieces]
        + [pltpu.VMEM((rows, width), BF), pltpu.SemaphoreType.DMA((len(pieces),))],
        flops=200_000_000,
        nbytes=6_000_000,
        limit=50,
    )
    others = [shift(normed, k) for k in range(1, n_mlp)]
    w_up, w_down, _ = lax.optimization_barrier((w_up, w_down, normed))
    w_up, w_down = call(
        load,
        (pltpu.VMEM(w_up.shape, BF), pltpu.VMEM(w_down.shape, BF)),
        (w_up, w_down),
        [HBM, HBM],
        [pltpu.SemaphoreType.DMA((2,))],
        nbytes=14_000_000,
        limit=50,
    )
    ys = call(
        mlp,
        (jax.ShapeDtypeStruct((rows, width), F32), row_bf, row_bf, row_bf),
        (normed, *others, w_gate, w_up, w_down),
        [VMEM] * 7,
        flops=700_000_000,
        nbytes=1_000_000,
        limit=14,
    )
    back = [shift(ys[k], -k) for k in range(1, n_mlp)]
    scores, hidden = call(
        finish,
        (jax.ShapeDtypeStruct((1, 2, 2, samp), F32), jax.ShapeDtypeStruct(residual.shape, BF)),
        (h1, ys[0], *back, norm_final[None], w_score[None]),
        [VMEM] * 7,
        flops=1_000_000,
        nbytes=500_000,
    )
    return (jnp.transpose(scores, (0, 1, 3, 2)), hidden, tails_out)


def solution(mesh):
    placed = (
        P("req", None, "mlp", None, None),
        P("req", None, "mlp", None, None),
        P("req", None, "mlp", None, None),
        P("req", None, None),
        P("req", "mlp", None, None),
        P(("req", "mlp"), None, None),
        P(("req", "mlp"), None),
        P(("req", "mlp"), None),
        P("req", None),
        P("req", None, "mlp"),
        P("mlp", None),
        P(),
        P(None, "mlp"),
        P(None, "mlp"),
        P("mlp", None),
        P(),
        P(),
    )
    return jax.shard_map(
        functools.partial(on_device, mesh.shape["req"], mesh.shape["mlp"]),
        mesh=mesh,
        in_specs=placed,
        out_specs=(
            P("req", None, "mlp", None),
            P("req", None, "mlp", None, None),
            P("req", None, "mlp", None, None),
        ),
        check_vma=False,
    )
```

```python
import functools

import jax
import jax.numpy as jnp
from jax import lax
from jax.experimental import pallas as pl
from jax.experimental.pallas import tpu as pltpu
from jax.sharding import PartitionSpec as P

BF = jnp.bfloat16
F32 = jnp.float32
NEG = -1e30
VMEM = pl.BlockSpec(memory_space=pltpu.VMEM)
SMEM = pl.BlockSpec(memory_space=pltpu.SMEM)
HBM = pl.BlockSpec(memory_space=pltpu.HBM)


def call(body, outs, operands, specs, scratch=(), flops=0, nbytes=0, limit=8, out_specs=None):
    return pl.pallas_call(
        body,
        out_shape=outs,
        in_specs=specs,
        out_specs=jax.tree.map(lambda _: VMEM, outs) if out_specs is None else out_specs,
        scratch_shapes=scratch,
        cost_estimate=pl.CostEstimate(flops=flops, bytes_accessed=nbytes, transcendentals=0),
        compiler_params=pltpu.CompilerParams(vmem_limit_bytes=limit << 20),
    )(*operands)


def iota(shape, axis):
    return lax.broadcasted_iota(jnp.int32, shape, axis)


def pick_pages(pool_ref, slot_ref, out_ref, scr):
    rows, slots, width = pool_ref.shape
    dests = slot_ref.shape[1]
    half = width // 2
    hot = (iota((slots, dests), 0) == slot_ref[...]).astype(F32).T.astype(BF)
    for i in range(rows):
        got = jnp.dot(hot, pool_ref[i], preferred_element_type=F32)
        scr[pl.ds(i, dests, stride=2 * rows), :] = got[:, :half]
        scr[pl.ds(rows + i, dests, stride=2 * rows), :] = got[:, half:]
    out_ref[...] = scr[...].astype(BF)


def load_rows(ref, q):
    parts = [ref[0, q, s].astype(F32) for s in range(ref.shape[2])]
    return jnp.concatenate(parts, axis=0)


def stack_heads(q8, size):
    heads = q8.shape[1] // size
    parts = [q8[:, h * size : (h + 1) * size] for h in range(heads)]
    return jnp.concatenate(parts, axis=0).astype(BF)


def row_lengths(tlen_ref, q, count):
    r = iota((2 * count, 1), 0)
    sample, token = r >> 1, r & 1
    length = jnp.zeros((2 * count, 1), jnp.int32)
    for s in range(count):
        length = jnp.where(sample == s, tlen_ref[0, q, s], length)
    return sample, token, length


def to_bias(visible):
    return jnp.where(visible, 0.0, NEG).astype(F32)


def window_bias(pos, plen, win, tail, sample, token, length):
    back = pos - win
    in_win = (pos < win) & (pos >= win - plen) & (pos > length + token)
    first = sample * tail
    in_tail = (back >= first) & (back < first + length)
    return to_bias(in_win | in_tail)


def new_bias(sample, token, count):
    c = iota((1, 2 * count), 1)
    return to_bias(((c >> 1) == sample) & ((c & 1) <= token))


def attend(qh, segments, rows, size):
    scale = 1.0 / jnp.sqrt(F32(size))
    heads = qh.shape[0] // rows
    scored = []
    top = None
    for keys, _, bias, _ in segments:
        s = lax.dot_general(qh, keys, (((1,), (1,)), ((), ())), preferred_element_type=F32)
        n = s.shape[1]
        s = s.reshape(heads, rows, n) * scale + bias[None]
        s = s.reshape(heads * rows, n)
        scored.append(s)
        m = s.max(axis=1, keepdims=True)
        top = m if top is None else jnp.maximum(top, m)
    total = None
    acc = None
    for s, (_, values, _, shift) in zip(scored, segments):
        e = jnp.exp(s - top)
        t = e.sum(axis=1, keepdims=True)
        if shift:
            e = pltpu.roll(e, shift, axis=1)
        o = jnp.dot(e.astype(BF), values, preferred_element_type=F32)
        total = t if total is None else total + t
        acc = o if acc is None else acc + o
    acc = acc / total
    return jnp.concatenate([acc[h * rows : (h + 1) * rows] for h in range(heads)], axis=1)


def resident(win, tail, size, page, n, q_ref, new_ref, kv_ref, tails_ref, holder_ref, plen_ref, tlen_ref, res_ref, out_ref):
    count = q_ref.shape[2]
    rows = 2 * count
    sample, token, length = row_lengths(tlen_ref, 0, count)
    q8 = load_rows(q_ref, 0)
    qh = stack_heads(q8, size)
    fresh = load_rows(new_ref, 0).astype(BF)
    tails = tails_ref[0].reshape(count * tail, 2 * size)
    window = kv_ref[0]
    wb = window_bias(iota((1, win), 1), plen_ref[0, 0], win, tail, sample, token, length)
    tb = window_bias(win + iota((1, count * tail), 1), plen_ref[0, 0], win, tail, sample, token, length)
    nb = new_bias(sample, token, count)
    out = attend(
        qh,
        [
            (window[:, :size], window[:, size:], wb, 0),
            (tails[:, :size], tails[:, size:], tb, 0),
            (fresh[:, :size], fresh[:, size:], nb, 0),
        ],
        rows,
        size,
    )
    c = iota((1, n), 1)
    pages = holder_ref.shape[1]
    per = n // pages
    origin = (c * (-(-(1 << 21) // per))) >> 21
    inside = c - origin * per
    base = jnp.zeros((1, n), jnp.int32)
    for p in range(pages):
        base = jnp.where(origin == holder_ref[0, p], p * page, base)
    pos = jnp.where(inside < page, base + inside, 1 << 20)
    sample, token, length = row_lengths(tlen_ref, 1, count)
    bias = window_bias(pos, plen_ref[0, 1], win, tail, sample, token, length)
    parts = (bias, load_rows(q_ref, 1), load_rows(new_ref, 1), load_rows(res_ref, 0), load_rows(res_ref, 1), out)
    out_ref[...] = jnp.concatenate(parts, axis=1).astype(BF)


def moved(size, page, arr_ref, state, norm_ref, wown, *refs):
    count = len(refs) // 2 - 2
    hbm, (h1_ref, normed_ref), vmem, (attn, sems) = refs[:count], refs[count : count + 2], refs[count + 2 : -2], refs[-2:]
    copies = [pltpu.make_async_copy(a, b, sems.at[i]) for i, (a, b) in enumerate(zip(hbm, vmem))]
    for c in copies:
        c.start()
    near, far, part_a, part_b = vmem
    n, width = arr_ref.shape[0], attn.shape[1]
    rows = state.shape[0]
    bias = state[:, :n].astype(F32)
    at = [n + width + 2 * size + i * width for i in range(4)]
    q8, fresh = state[:, n : n + width], state[:, n + width : at[0]]
    res = jnp.concatenate([state[:, at[0] : at[1]], state[:, at[1] : at[2]]], axis=0).astype(F32)
    first = state[:, at[2] : at[3]].astype(F32)
    r = iota((rows, 1), 0)
    nb = new_bias(r >> 1, r & 1, rows // 2)
    arr = arr_ref[...]
    second = attend(
        stack_heads(q8.astype(F32), size),
        [(arr, arr, bias, page), (fresh[:, :size], fresh[:, size:], nb, 0)],
        rows,
        size,
    )
    for c in copies:
        c.wait()
    attn[...] = jnp.concatenate([first, second], axis=0).astype(BF)
    me = lax.axis_index("mlp")
    core = lax.rem(lax.axis_index("req"), 2)
    block = wown.shape[0]
    n_mlp = width // block
    part = part_a.shape[0]

    def piece(k):
        rb = lax.rem(me + k + n_mlp, n_mlp)
        return attn[:, pl.ds(pl.multiple_of(rb * block, 128), block)]

    def product(x, w):
        return jnp.dot(x, w[...], preferred_element_type=F32)

    opposite = piece(2).astype(F32)
    low, high = opposite[:, :part], opposite[:, part:]
    mixed = product(piece(0), wown) + product(piece(2 * core - 1), near) + product(piece(1 - 2 * core), far)
    mixed = mixed + product(jnp.where(core == 0, low, high).astype(BF), part_a)
    mixed = mixed + product(jnp.where(core == 0, high, low).astype(BF), part_b)
    h1 = (res + mixed).astype(BF)
    h1_ref[...] = h1
    f = h1.astype(F32)
    inv = lax.rsqrt(jnp.mean(f * f, axis=1, keepdims=True) + 1e-6)
    normed_ref[...] = (f * inv * norm_ref[...]).astype(BF)


def write_tails(win, page, arr_ref, tails_ref, new_ref, holder_ref, tlen_ref, out_ref, scr):
    count, tail, width = tails_ref.shape[1:]
    half = width // 2
    pages = holder_ref.shape[1]
    start = win // page
    lead = win - start * page
    for p in range(start, pages):
        block = arr_ref[holder_ref[0, p]].astype(F32)
        off = (p - start) * page
        scr[off : off + page, :half] = block[:page]
        scr[off : off + page, half:] = block[page:]
    row = iota((tail, 1), 0)
    for q in range(2):
        for s in range(count):
            if q == 0:
                old = tails_ref[0, s].astype(F32)
            else:
                old = scr[lead + s * tail : lead + (s + 1) * tail, :]
            fresh = new_ref[0, q, s].astype(F32)
            length = tlen_ref[0, q, s]
            t = jnp.where(row == length, fresh[0:1], old)
            t = jnp.where(row == length + 1, fresh[1:2], t)
            out_ref[0, q, s] = t.astype(BF)


def load(*refs):
    count = len(refs) // 2
    sems = refs[-1]
    copies = [pltpu.make_async_copy(refs[i], refs[count + i], sems.at[i]) for i in range(count)]
    for c in copies:
        c.start()
    for c in copies:
        c.wait()


def mlp(x0, x1, x2, x3, wg, wu, wd, y0, y1, y2, y3):
    x = jnp.concatenate([x0[...], x1[...], x2[...], x3[...]], axis=0)
    gate = jnp.dot(x, wg[...], preferred_element_type=F32)
    up = jnp.dot(x, wu[...], preferred_element_type=F32)
    act = (jax.nn.gelu(gate, approximate=True) * up).astype(BF)
    y = jnp.dot(act, wd[...], preferred_element_type=F32)
    n = x0.shape[0]
    y0[...] = y[:n]
    y1[...] = y[n : 2 * n].astype(BF)
    y2[...] = y[2 * n : 3 * n].astype(BF)
    y3[...] = y[3 * n :].astype(BF)


def finish(h1_ref, y0, y1, y2, y3, nf_ref, ws_ref, score_ref, hid_ref):
    h2 = h1_ref[...].astype(F32) + (y0[...] + y1[...].astype(F32) + y2[...].astype(F32) + y3[...].astype(F32))
    inv = lax.rsqrt(jnp.mean(h2 * h2, axis=1, keepdims=True) + 1e-6)
    sc = jnp.sum(h2 * inv * nf_ref[...] * ws_ref[...], axis=1, keepdims=True)
    n = h2.shape[0]
    count = n // 4
    row, col = iota((n, count), 0), iota((n, count), 1)
    for q in range(2):
        for t in range(2):
            hit = row == q * 2 * count + col * 2 + t
            score_ref[0, q, t : t + 1, :] = jnp.sum(jnp.where(hit, sc, 0.0), axis=0, keepdims=True)
        for s in range(count):
            r = q * 2 * count + s * 2
            hid_ref[0, q, s] = h2[r : r + 2].astype(BF)


def on_device(
    n_req,
    n_mlp,
    queries,
    new_kv,
    residual,
    prompt_kv,
    tail_kv,
    page_pool,
    page_holder,
    serve_slot,
    prompt_len,
    tail_len,
    w_out,
    norm_mlp,
    w_gate,
    w_up,
    w_down,
    norm_final,
    w_score,
):
    samp, width = residual.shape[2], residual.shape[-1]
    size = new_kv.shape[-1] // 2
    win, tail = prompt_kv.shape[1], tail_kv.shape[2]
    slots, page = page_pool.shape[:2]
    rows = 4 * samp
    arrived_rows = n_req * 2 * page
    block, hid = w_out.shape[0], w_gate.shape[1]
    part = block // 2

    def shift(x, k):
        return lax.ppermute(x, "mlp", [(i, (i + k) % n_mlp) for i in range(n_mlp)])

    def swap(x):
        return lax.ppermute(x, "req", [(i, i ^ 1) for i in range(n_req)])

    def onward(x):
        to = [(r * n_mlp + m, r * n_mlp + (m + 1 - 2 * (r % 2)) % n_mlp) for r in range(n_req) for m in range(n_mlp)]
        return lax.ppermute(x, ("req", "mlp"), to)

    near = onward(w_out)
    outgoing = call(
        pick_pages,
        jax.ShapeDtypeStruct((arrived_rows, size), BF),
        (jnp.transpose(page_pool, (1, 0, 2)), serve_slot),
        [VMEM, VMEM],
        [pltpu.VMEM((arrived_rows, size), F32)],
        flops=100_000_000,
        nbytes=1_400_000,
        limit=60,
    )
    arrived = lax.all_to_all(
        outgoing.reshape(n_req, 2 * page, size), "req", split_axis=0, concat_axis=0, tiled=True
    )
    q_late, outgoing = lax.optimization_barrier((queries, outgoing))
    state = call(
        functools.partial(resident, win, tail, size, page, arrived_rows),
        jax.ShapeDtypeStruct((2 * samp, arrived_rows + 4 * width + 2 * size), BF),
        (q_late, new_kv, prompt_kv, tail_kv, page_holder, prompt_len, tail_len, residual),
        [VMEM, VMEM, VMEM, VMEM, SMEM, SMEM, SMEM, VMEM],
        flops=100_000_000,
        nbytes=1_000_000,
        limit=40,
    )
    core = lax.rem(lax.axis_index("req"), 2)
    part_a = onward(lax.dynamic_slice_in_dim(near, core * part, part, 0))
    far, part_b = swap(near), swap(part_a)
    tails_out = call(
        functools.partial(write_tails, win, page),
        jax.ShapeDtypeStruct((1, 2) + tail_kv.shape[1:], BF),
        (arrived, tail_kv, new_kv, page_holder, tail_len),
        [VMEM, VMEM, VMEM, SMEM, SMEM],
        [pltpu.VMEM(((n_req - win // page) * page, 2 * size), F32)],
        flops=1_000_000,
        nbytes=1_500_000,
    )
    pieces = (near, far, part_a, part_b)
    row_bf = jax.ShapeDtypeStruct((rows, width), BF)
    h1, normed = call(
        functools.partial(moved, size, page),
        (row_bf, row_bf),
        (arrived.reshape(arrived_rows, size), state, norm_mlp[None], w_out, *pieces),
        [VMEM] * 4 + [HBM] * len(pieces),
        [pltpu.VMEM(x.shape, x.dtype) for x in pieces]
        + [pltpu.VMEM((rows, width), BF), pltpu.SemaphoreType.DMA((len(pieces),))],
        flops=200_000_000,
        nbytes=6_000_000,
        limit=50,
    )
    others = [shift(normed, k) for k in range(1, n_mlp)]
    w_up, w_down, _ = lax.optimization_barrier((w_up, w_down, normed))
    w_up, w_down = call(
        load,
        (pltpu.VMEM(w_up.shape, BF), pltpu.VMEM(w_down.shape, BF)),
        (w_up, w_down),
        [HBM, HBM],
        [pltpu.SemaphoreType.DMA((2,))],
        nbytes=14_000_000,
        limit=50,
    )
    ys = call(
        mlp,
        (jax.ShapeDtypeStruct((rows, width), F32), row_bf, row_bf, row_bf),
        (normed, *others, w_gate, w_up, w_down),
        [VMEM] * 7,
        flops=700_000_000,
        nbytes=1_000_000,
        limit=14,
    )
    back = [shift(ys[k], -k) for k in range(1, n_mlp)]
    scores, hidden = call(
        finish,
        (jax.ShapeDtypeStruct((1, 2, 2, samp), F32), jax.ShapeDtypeStruct(residual.shape, BF)),
        (h1, ys[0], *back, norm_final[None], w_score[None]),
        [VMEM] * 7,
        flops=1_000_000,
        nbytes=500_000,
    )
    return (jnp.transpose(scores, (0, 1, 3, 2)), hidden, tails_out)


def solution(mesh):
    placed = (
        P("req", None, "mlp", None, None),
        P("req", None, "mlp", None, None),
        P("req", None, "mlp", None, None),
        P("req", None, None),
        P("req", "mlp", None, None),
        P(("req", "mlp"), None, None),
        P(("req", "mlp"), None),
        P(("req", "mlp"), None),
        P("req", None),
        P("req", None, "mlp"),
        P("mlp", None),
        P(),
        P(None, "mlp"),
        P(None, "mlp"),
        P("mlp", None),
        P(),
        P(),
    )
    return jax.shard_map(
        functools.partial(on_device, mesh.shape["req"], mesh.shape["mlp"]),
        mesh=mesh,
        in_specs=placed,
        out_specs=(
            P("req", None, "mlp", None),
            P("req", None, "mlp", None, None),
            P("req", None, "mlp", None, None),
        ),
        check_vma=False,
    )
```

```python
import functools
import math

import jax
import jax.numpy as jnp
from jax import lax
from jax.experimental import pallas as pl
from jax.experimental.pallas import tpu as pltpu
from jax.sharding import PartitionSpec as P

BF = jnp.bfloat16
F32 = jnp.float32
NEG = -1e30
VMEM = pl.BlockSpec(memory_space=pltpu.VMEM)
SMEM = pl.BlockSpec(memory_space=pltpu.SMEM)
HBM = pl.BlockSpec(memory_space=pltpu.HBM)


def call(body, outs, operands, specs, scratch=(), flops=0, nbytes=0, limit=8, out_specs=None):
    return pl.pallas_call(
        body,
        out_shape=outs,
        in_specs=specs,
        out_specs=jax.tree.map(lambda _: VMEM, outs) if out_specs is None else out_specs,
        scratch_shapes=scratch,
        cost_estimate=pl.CostEstimate(flops=flops, bytes_accessed=nbytes, transcendentals=0),
        compiler_params=pltpu.CompilerParams(vmem_limit_bytes=limit << 20),
    )(*operands)


def iota(shape, axis):
    return lax.broadcasted_iota(jnp.int32, shape, axis)


def pick_pages(pool_ref, slot_ref, out_ref, scr):
    rows, slots, width = pool_ref.shape
    dests = slot_ref.shape[1]
    half = width // 2
    hot = (iota((slots, dests), 0) == slot_ref[...]).astype(F32).T.astype(BF)
    for i in range(rows):
        got = jnp.dot(hot, pool_ref[i], preferred_element_type=F32)
        scr[pl.ds(i, dests, stride=2 * rows), :] = got[:, :half]
        scr[pl.ds(rows + i, dests, stride=2 * rows), :] = got[:, half:]
    out_ref[...] = scr[...].astype(BF)


def load_rows(ref, q):
    parts = [ref[0, q, s].astype(F32) for s in range(ref.shape[2])]
    return jnp.concatenate(parts, axis=0)


def stack_heads(q8, size):
    heads = q8.shape[1] // size
    parts = [q8[:, h * size : (h + 1) * size] for h in range(heads)]
    return jnp.concatenate(parts, axis=0).astype(BF)


def row_lengths(tlen_ref, q, count):
    r = iota((2 * count, 1), 0)
    sample, token = r >> 1, r & 1
    length = jnp.zeros((2 * count, 1), jnp.int32)
    for s in range(count):
        length = jnp.where(sample == s, tlen_ref[0, q, s], length)
    return sample, token, length


def to_bias(visible):
    return jnp.where(visible, 0.0, NEG).astype(F32)


def window_bias(pos, plen, win, tail, sample, token, length):
    back = pos - win
    in_win = (pos < win) & (pos >= win - plen) & (pos > length + token)
    first = sample * tail
    in_tail = (back >= first) & (back < first + length)
    return to_bias(in_win | in_tail)


def new_bias(sample, token, count):
    c = iota((1, 2 * count), 1)
    return to_bias(((c >> 1) == sample) & ((c & 1) <= token))


def attend(qh, segments, rows, size):
    scale = F32(math.log2(math.e) / math.sqrt(size))
    heads = qh.shape[0] // rows
    scored = []
    top = None
    for keys, _, bias, _ in segments:
        s = lax.dot_general(qh, keys, (((1,), (1,)), ((), ())), preferred_element_type=F32)
        n = s.shape[1]
        s = s.reshape(heads, rows, n) * scale + bias[None]
        s = s.reshape(heads * rows, n)
        scored.append(s)
        m = s.max(axis=1, keepdims=True)
        top = m if top is None else jnp.maximum(top, m)
    total = None
    acc = None
    for s, (_, values, _, shift) in zip(scored, segments):
        e = jnp.exp2(s - top)
        t = e.sum(axis=1, keepdims=True)
        if shift:
            e = pltpu.roll(e, shift, axis=1)
        o = jnp.dot(e.astype(BF), values, preferred_element_type=F32)
        total = t if total is None else total + t
        acc = o if acc is None else acc + o
    acc = acc / total
    return jnp.concatenate([acc[h * rows : (h + 1) * rows] for h in range(heads)], axis=1)


def resident(win, tail, size, page, n, q_ref, new_ref, kv_ref, tails_ref, holder_ref, plen_ref, tlen_ref, res_ref, out_ref):
    count = q_ref.shape[2]
    rows = 2 * count
    sample, token, length = row_lengths(tlen_ref, 0, count)
    q8 = load_rows(q_ref, 0)
    qh = stack_heads(q8, size)
    fresh = load_rows(new_ref, 0).astype(BF)
    tails = tails_ref[0].reshape(count * tail, 2 * size)
    window = kv_ref[0]
    wb = window_bias(iota((1, win), 1), plen_ref[0, 0], win, tail, sample, token, length)
    tb = window_bias(win + iota((1, count * tail), 1), plen_ref[0, 0], win, tail, sample, token, length)
    nb = new_bias(sample, token, count)
    out = attend(
        qh,
        [
            (window[:, :size], window[:, size:], wb, 0),
            (tails[:, :size], tails[:, size:], tb, 0),
            (fresh[:, :size], fresh[:, size:], nb, 0),
        ],
        rows,
        size,
    )
    c = iota((1, n), 1)
    pages = holder_ref.shape[1]
    per = n // pages
    origin = (c * (-(-(1 << 21) // per))) >> 21
    inside = c - origin * per
    base = jnp.zeros((1, n), jnp.int32)
    for p in range(pages):
        base = jnp.where(origin == holder_ref[0, p], p * page, base)
    pos = jnp.where(inside < page, base + inside, 1 << 20)
    sample, token, length = row_lengths(tlen_ref, 1, count)
    bias = window_bias(pos, plen_ref[0, 1], win, tail, sample, token, length)
    parts = (bias, load_rows(q_ref, 1), load_rows(new_ref, 1), load_rows(res_ref, 0), load_rows(res_ref, 1), out)
    out_ref[...] = jnp.concatenate(parts, axis=1).astype(BF)


def moved(size, page, arr_ref, state, norm_ref, wown, *refs):
    count = len(refs) // 2 - 2
    hbm, (h1_ref, normed_ref), vmem, (attn, sems) = refs[:count], refs[count : count + 2], refs[count + 2 : -2], refs[-2:]
    copies = [pltpu.make_async_copy(a, b, sems.at[i]) for i, (a, b) in enumerate(zip(hbm, vmem))]
    for c in copies:
        c.start()
    near, far, part_a, part_b = vmem
    n, width = arr_ref.shape[0], attn.shape[1]
    rows = state.shape[0]
    bias = state[:, :n].astype(F32)
    at = [n + width + 2 * size + i * width for i in range(4)]
    q8, fresh = state[:, n : n + width], state[:, n + width : at[0]]
    res = jnp.concatenate([state[:, at[0] : at[1]], state[:, at[1] : at[2]]], axis=0).astype(F32)
    first = state[:, at[2] : at[3]].astype(F32)
    r = iota((rows, 1), 0)
    nb = new_bias(r >> 1, r & 1, rows // 2)
    arr = arr_ref[...]
    second = attend(
        stack_heads(q8.astype(F32), size),
        [(arr, arr, bias, page), (fresh[:, :size], fresh[:, size:], nb, 0)],
        rows,
        size,
    )
    for c in copies:
        c.wait()
    attn[...] = jnp.concatenate([first, second], axis=0).astype(BF)
    me = lax.axis_index("mlp")
    core = lax.rem(lax.axis_index("req"), 2)
    block = wown.shape[0]
    n_mlp = width // block
    part = part_a.shape[0]

    def piece(k):
        rb = lax.rem(me + k + n_mlp, n_mlp)
        return attn[:, pl.ds(pl.multiple_of(rb * block, 128), block)]

    def product(x, w):
        return jnp.dot(x, w[...], preferred_element_type=F32)

    opposite = piece(2).astype(F32)
    low, high = opposite[:, :part], opposite[:, part:]
    mixed = product(piece(0), wown) + product(piece(2 * core - 1), near) + product(piece(1 - 2 * core), far)
    mixed = mixed + product(jnp.where(core == 0, low, high).astype(BF), part_a)
    mixed = mixed + product(jnp.where(core == 0, high, low).astype(BF), part_b)
    h1 = (res + mixed).astype(BF)
    h1_ref[...] = h1
    f = h1.astype(F32)
    inv = lax.rsqrt(jnp.mean(f * f, axis=1, keepdims=True) + 1e-6)
    normed_ref[...] = (f * inv * norm_ref[...]).astype(BF)


def write_tails(win, page, arr_ref, tails_ref, new_ref, holder_ref, tlen_ref, out_ref, scr):
    count, tail, width = tails_ref.shape[1:]
    half = width // 2
    pages = holder_ref.shape[1]
    start = win // page
    lead = win - start * page
    for p in range(start, pages):
        block = arr_ref[holder_ref[0, p]].astype(F32)
        off = (p - start) * page
        scr[off : off + page, :half] = block[:page]
        scr[off : off + page, half:] = block[page:]
    row = iota((tail, 1), 0)
    for q in range(2):
        for s in range(count):
            if q == 0:
                old = tails_ref[0, s].astype(F32)
            else:
                old = scr[lead + s * tail : lead + (s + 1) * tail, :]
            fresh = new_ref[0, q, s].astype(F32)
            length = tlen_ref[0, q, s]
            t = jnp.where(row == length, fresh[0:1], old)
            t = jnp.where(row == length + 1, fresh[1:2], t)
            out_ref[0, q, s] = t.astype(BF)


def load(*refs):
    count = len(refs) // 2
    sems = refs[-1]
    copies = [pltpu.make_async_copy(refs[i], refs[count + i], sems.at[i]) for i in range(count)]
    for c in copies:
        c.start()
    for c in copies:
        c.wait()


def mlp(x0, x1, x2, x3, wg, wu, wd, y0, y1, y2, y3):
    x = jnp.concatenate([x0[...], x1[...], x2[...], x3[...]], axis=0)
    gate = jnp.dot(x, wg[...], preferred_element_type=F32)
    up = jnp.dot(x, wu[...], preferred_element_type=F32)
    act = (jax.nn.gelu(gate, approximate=True) * up).astype(BF)
    y = jnp.dot(act, wd[...], preferred_element_type=F32)
    n = x0.shape[0]
    y0[...] = y[:n]
    y1[...] = y[n : 2 * n].astype(BF)
    y2[...] = y[2 * n : 3 * n].astype(BF)
    y3[...] = y[3 * n :].astype(BF)


def finish(h1_ref, y0, y1, y2, y3, nf_ref, ws_ref, score_ref, hid_ref):
    h2 = h1_ref[...].astype(F32) + (y0[...] + y1[...].astype(F32) + y2[...].astype(F32) + y3[...].astype(F32))
    inv = lax.rsqrt(jnp.mean(h2 * h2, axis=1, keepdims=True) + 1e-6)
    sc = jnp.sum(h2 * inv * nf_ref[...] * ws_ref[...], axis=1, keepdims=True)
    n = h2.shape[0]
    count = n // 4
    row, col = iota((n, count), 0), iota((n, count), 1)
    for q in range(2):
        for t in range(2):
            hit = row == q * 2 * count + col * 2 + t
            score_ref[0, q, t : t + 1, :] = jnp.sum(jnp.where(hit, sc, 0.0), axis=0, keepdims=True)
        for s in range(count):
            r = q * 2 * count + s * 2
            hid_ref[0, q, s] = h2[r : r + 2].astype(BF)


def on_device(
    n_req,
    n_mlp,
    queries,
    new_kv,
    residual,
    prompt_kv,
    tail_kv,
    page_pool,
    page_holder,
    serve_slot,
    prompt_len,
    tail_len,
    w_out,
    norm_mlp,
    w_gate,
    w_up,
    w_down,
    norm_final,
    w_score,
):
    samp, width = residual.shape[2], residual.shape[-1]
    size = new_kv.shape[-1] // 2
    win, tail = prompt_kv.shape[1], tail_kv.shape[2]
    slots, page = page_pool.shape[:2]
    rows = 4 * samp
    arrived_rows = n_req * 2 * page
    block, hid = w_out.shape[0], w_gate.shape[1]
    part = block // 2

    def shift(x, k):
        return lax.ppermute(x, "mlp", [(i, (i + k) % n_mlp) for i in range(n_mlp)])

    def swap(x):
        return lax.ppermute(x, "req", [(i, i ^ 1) for i in range(n_req)])

    def onward(x):
        to = [(r * n_mlp + m, r * n_mlp + (m + 1 - 2 * (r % 2)) % n_mlp) for r in range(n_req) for m in range(n_mlp)]
        return lax.ppermute(x, ("req", "mlp"), to)

    near = onward(w_out)
    outgoing = call(
        pick_pages,
        jax.ShapeDtypeStruct((arrived_rows, size), BF),
        (jnp.transpose(page_pool, (1, 0, 2)), serve_slot),
        [VMEM, VMEM],
        [pltpu.VMEM((arrived_rows, size), F32)],
        flops=100_000_000,
        nbytes=1_400_000,
        limit=60,
    )
    arrived = lax.all_to_all(
        outgoing.reshape(n_req, 2 * page, size), "req", split_axis=0, concat_axis=0, tiled=True
    )
    q_late, outgoing = lax.optimization_barrier((queries, outgoing))
    state = call(
        functools.partial(resident, win, tail, size, page, arrived_rows),
        jax.ShapeDtypeStruct((2 * samp, arrived_rows + 4 * width + 2 * size), BF),
        (q_late, new_kv, prompt_kv, tail_kv, page_holder, prompt_len, tail_len, residual),
        [VMEM, VMEM, VMEM, VMEM, SMEM, SMEM, SMEM, VMEM],
        flops=100_000_000,
        nbytes=1_000_000,
        limit=40,
    )
    core = lax.rem(lax.axis_index("req"), 2)
    part_a = onward(lax.dynamic_slice_in_dim(near, core * part, part, 0))
    far, part_b = swap(near), swap(part_a)
    tails_out = call(
        functools.partial(write_tails, win, page),
        jax.ShapeDtypeStruct((1, 2) + tail_kv.shape[1:], BF),
        (arrived, tail_kv, new_kv, page_holder, tail_len),
        [VMEM, VMEM, VMEM, SMEM, SMEM],
        [pltpu.VMEM(((n_req - win // page) * page, 2 * size), F32)],
        flops=1_000_000,
        nbytes=1_500_000,
    )
    pieces = (near, far, part_a, part_b)
    row_bf = jax.ShapeDtypeStruct((rows, width), BF)
    h1, normed = call(
        functools.partial(moved, size, page),
        (row_bf, row_bf),
        (arrived.reshape(arrived_rows, size), state, norm_mlp[None], w_out, *pieces),
        [VMEM] * 4 + [HBM] * len(pieces),
        [pltpu.VMEM(x.shape, x.dtype) for x in pieces]
        + [pltpu.VMEM((rows, width), BF), pltpu.SemaphoreType.DMA((len(pieces),))],
        flops=200_000_000,
        nbytes=6_000_000,
        limit=50,
    )
    others = [shift(normed, k) for k in range(1, n_mlp)]
    w_up, w_down, _ = lax.optimization_barrier((w_up, w_down, normed))
    w_up, w_down = call(
        load,
        (pltpu.VMEM(w_up.shape, BF), pltpu.VMEM(w_down.shape, BF)),
        (w_up, w_down),
        [HBM, HBM],
        [pltpu.SemaphoreType.DMA((2,))],
        nbytes=14_000_000,
        limit=50,
    )
    ys = call(
        mlp,
        (jax.ShapeDtypeStruct((rows, width), F32), row_bf, row_bf, row_bf),
        (normed, *others, w_gate, w_up, w_down),
        [VMEM] * 7,
        flops=700_000_000,
        nbytes=1_000_000,
        limit=14,
    )
    back = [shift(ys[k], -k) for k in range(1, n_mlp)]
    scores, hidden = call(
        finish,
        (jax.ShapeDtypeStruct((1, 2, 2, samp), F32), jax.ShapeDtypeStruct(residual.shape, BF)),
        (h1, ys[0], *back, norm_final[None], w_score[None]),
        [VMEM] * 7,
        flops=1_000_000,
        nbytes=500_000,
    )
    return (jnp.transpose(scores, (0, 1, 3, 2)), hidden, tails_out)


def solution(mesh):
    placed = (
        P("req", None, "mlp", None, None),
        P("req", None, "mlp", None, None),
        P("req", None, "mlp", None, None),
        P("req", None, None),
        P("req", "mlp", None, None),
        P(("req", "mlp"), None, None),
        P(("req", "mlp"), None),
        P(("req", "mlp"), None),
        P("req", None),
        P("req", None, "mlp"),
        P("mlp", None),
        P(),
        P(None, "mlp"),
        P(None, "mlp"),
        P("mlp", None),
        P(),
        P(),
    )
    return jax.shard_map(
        functools.partial(on_device, mesh.shape["req"], mesh.shape["mlp"]),
        mesh=mesh,
        in_specs=placed,
        out_specs=(
            P("req", None, "mlp", None),
            P("req", None, "mlp", None, None),
            P("req", None, "mlp", None, None),
        ),
        check_vma=False,
    )
```
